32 devices in a mesh: dp: 16 (over z, y, x), tensor: 2 (over core).
Axes of the slice: x: 2, y: 2, z: 4, core: 2. Of those that a mesh axis runs over, the one named last changes fastest.
Arguments:
- tokens: bfloat16 [4096, 768], P('dp'), may hold values from -6 to 6
- cotangent: bfloat16 [4096, 768], P('dp'), may hold values from -6 to 6
- packing: int32 [4096], replicated, may hold values from 0 to 4095, as said below
- lengths: int32 [32, 4], P('dp'), may hold values from 0 to 128, as said below
- labels: int32 [128], P('dp'), may hold values from 0 to 1
- w_qkv: bfloat16 [2, 3, 768, 768], P(None, None, 'dp', 'tensor'), may hold values from -0.21875 to 0.21875
- b_qv: float32 [2, 2, 768], P(None, None, 'tensor'), may hold values from -3 to 3
- w_out: bfloat16 [2, 768, 768], P(None, 'tensor', 'dp'), may hold values from -1.25 to 1.25
- b_out: float32 [2, 768], replicated, may hold values from -3 to 3
- w_in: bfloat16 [2, 768, 3072], P(None, 'dp', 'tensor'), may hold values from -0.21875 to 0.21875
- b_in: float32 [2, 3072], P(None, 'tensor'), may hold values from -3 to 3
- w_down: bfloat16 [2, 3072, 768], P(None, 'tensor', 'dp'), may hold values from -0.109375 to 0.109375
- b_down: float32 [2, 768], replicated, may hold values from -3 to 3
- norm_gains: float32 [2, 2, 768], replicated, may hold values from 0.5 to 1.5
- norm_shifts: float32 [2, 2, 768], replicated, may hold values from -3 to 3
- pool_w: bfloat16 [2, 768, 768], P(None, 'dp'), may hold values from -0.21875 to 0.21875
- pool_b: float32 [2, 768], replicated, may hold values from -3 to 3
- cls_w: float32 [2, 768, 2], replicated, may hold values from -0.4375 to 0.4375
- cls_b: float32 [2, 2], replicated, may hold values from -3 to 3
Outputs:
- block_out: bfloat16 [4096, 768], P('dp')
- exits: float32 [2, 128, 2], P(None, 'dp')
- tokens_grad: bfloat16 [4096, 768], P('dp')
- w_qkv_grad: float32 [2, 3, 768, 768], P(None, None, 'dp', 'tensor')
- b_qv_grad: float32 [2, 2, 768], P(None, None, 'tensor')
- w_out_grad: float32 [2, 768, 768], P(None, 'tensor', 'dp')
- b_out_grad: float32 [2, 768], replicated
- w_in_grad: float32 [2, 768, 3072], P(None, 'dp', 'tensor')
- b_in_grad: float32 [2, 3072], P(None, 'tensor')
- w_down_grad: float32 [2, 3072, 768], P(None, 'tensor', 'dp')
- b_down_grad: float32 [2, 768], replicated
- norm_gains_grad: float32 [2, 2, 768], replicated
- norm_shifts_grad: float32 [2, 2, 768], replicated
- pool_w_grad: float32 [2, 768, 768], P(None, 'dp')
- pool_b_grad: float32 [2, 768], replicated
- cls_w_grad: float32 [2, 768, 2], replicated
- cls_b_grad: float32 [2, 2], replicated
The draws below stay inside these ranges and needn't reach their ends.
Inputs may be any that keep to these rules, and one draw needn't show every extreme that they name: packing is a permutation: token r goes to packed position packing[r] of data group packing[r] // 256; the 256 tokens of every data group's input send exactly 16 tokens to each data group. The 4 lengths of every micro-batch sum to 128; in every draw some micro-batch holds one sequence of all 128 rows.
All inputs are finite; a program needn't handle non-finite values.
Results may differ from the reference program's by a relative error of at most 0.04.
Values may be sent and summed in bfloat16 or wider, within the bound.
No kernel may reach another device: no remote copies, remote signals or barrier semaphores. Data moves between devices by JAX's collectives and lax.ppermute only.
A program may use at most 192 MiB of HBM per device.

```python
import jax
import jax.numpy as jnp
from jax import lax

D = 768
HEAD = 64
FF = 3072
CLASSES = 2
LAYERS = 2
SLOTS = 4
TOK_MB = 128
GROUPS = 2
TOK_DEV = 256
TOKENS = 4096
BATCHES = 32
NSEQ = 128
SHARE = 16


def draw_packing(key, part):
    groups_count = TOKENS // TOK_DEV
    row_keys = jax.random.split(jax.random.fold_in(key, 11), groups_count)
    slot_keys = jax.random.split(jax.random.fold_in(key, 12), groups_count)
    row_perms = jax.vmap(lambda one_key: jax.random.permutation(one_key, TOK_DEV))(row_keys).astype(jnp.int32)
    slot_perms = jax.vmap(lambda one_key: jax.random.permutation(one_key, TOK_DEV))(slot_keys).astype(jnp.int32)
    source = jnp.arange(groups_count, dtype=jnp.int32)[:, None, None]
    target = jnp.arange(groups_count, dtype=jnp.int32)[None, :, None]
    within = jnp.arange(SHARE, dtype=jnp.int32)[None, None, :]
    natural = source * TOK_DEV + row_perms[source, target * SHARE + within]
    packed = target * TOK_DEV + slot_perms[target, source * SHARE + within]
    return jnp.zeros((TOKENS,), jnp.int32).at[natural.reshape(-1)].set(packed.reshape(-1).astype(jnp.int32))


def draw_lengths(key, part):
    cuts = jax.random.randint(jax.random.fold_in(key, 21), (BATCHES, SLOTS - 1), 0, TOK_MB + 1).astype(jnp.int32)
    cuts = jnp.sort(cuts, axis=1)
    edges = jnp.concatenate([jnp.zeros((BATCHES, 1), jnp.int32), cuts, jnp.full((BATCHES, 1), TOK_MB, jnp.int32)], axis=1)
    spans = edges[:, 1:] - edges[:, :-1]
    chosen = jax.random.randint(jax.random.fold_in(key, 22), (), 0, BATCHES)
    single = jnp.where(jnp.arange(SLOTS) == 0, TOK_MB, 0).astype(jnp.int32)
    return jnp.where((jnp.arange(BATCHES) == chosen)[:, None], single[None, :], spans).astype(jnp.int32)


def touch_ends(entries, rng, smallest, largest):
    longest = entries.shape.index(max(entries.shape))
    spots = []
    for shift in (0, 1):
        where = [jax.random.randint(jax.random.fold_in(rng, axis), (), 0, length) for axis, length in enumerate(entries.shape)]
        where[longest] = (where[longest] + shift) % entries.shape[longest]
        spots.append(tuple(where))
    return entries.at[spots[0]].set(smallest).at[spots[1]].set(largest)


def levels(key, extent, pieces, least, largest):
    factor_of = 1.0
    for axis_at, shards_of in pieces:
        draws = jax.random.uniform(jax.random.fold_in(jax.random.fold_in(key, 6), axis_at), (shards_of,), jnp.float32, least / len(pieces), largest / len(pieces))
        factor_of = factor_of * jnp.repeat(jnp.exp(draws), extent[axis_at] // shards_of).reshape((-1,) + (1,) * (len(extent) - 1 - axis_at))
    return factor_of


def noise(stream_key, shape, scale, bound, cuts=(), kind=jnp.bfloat16):
    entries = scale * jax.random.normal(stream_key, shape, jnp.float32)
    if cuts:
        entries = entries * levels(stream_key, shape, cuts, -0.22, 0.18)
    return jnp.clip(entries, -bound, bound).astype(kind)


def setup_inputs(seed: int = 0) -> dict:
    key_list = jax.random.split(jax.random.key(seed), 20)
    return {
        "tokens": noise(key_list[0], (TOKENS, D), 1.0, 6.0, ((0, 16),)),
        "cotangent": noise(key_list[1], (TOKENS, D), 1.0, 6.0, ((0, 16),)),
        "packing": draw_packing(jax.random.fold_in(key_list[19], 71), 0),
        "lengths": draw_lengths(jax.random.fold_in(key_list[19], 71), 0),
        "labels": touch_ends(jax.random.randint(key_list[4], (NSEQ,), 0, CLASSES), jax.random.fold_in(key_list[4], 1), 0, CLASSES - 1).astype(jnp.int32),
        "w_qkv": noise(key_list[5], (LAYERS, 3, D, D), D ** -0.5, 0.21875, ((2, 16), (3, 2))),
        "b_qv": noise(key_list[6], (LAYERS, 2, D), 0.5, 3.0, ((2, 2),), jnp.float32),
        "w_out": noise(key_list[7], (LAYERS, D, D), (D // 32) ** -0.5, 1.25, ((1, 2), (2, 16))),
        "b_out": noise(key_list[8], (LAYERS, D), 0.5, 3.0, (), jnp.float32),
        "w_in": noise(key_list[9], (LAYERS, D, FF), D ** -0.5, 0.21875, ((1, 16), (2, 2))),
        "b_in": noise(key_list[10], (LAYERS, FF), 0.5, 3.0, ((1, 2),), jnp.float32),
        "w_down": noise(key_list[11], (LAYERS, FF, D), FF ** -0.5, 0.109375, ((1, 2), (2, 16))),
        "b_down": noise(key_list[12], (LAYERS, D), 0.5, 3.0, (), jnp.float32),
        "norm_gains": jnp.clip(1.0 + 0.1 * jax.random.normal(key_list[13], (LAYERS, 2, D), jnp.float32), 0.5, 1.5),
        "norm_shifts": noise(key_list[14], (LAYERS, 2, D), 0.5, 3.0, (), jnp.float32),
        "pool_w": noise(key_list[15], (LAYERS, D, D), D ** -0.5, 0.21875, ((1, 16),)),
        "pool_b": noise(key_list[16], (LAYERS, D), 0.5, 3.0, (), jnp.float32),
        "cls_w": noise(key_list[17], (LAYERS, D, CLASSES), (D // 4) ** -0.5, 0.4375, (), jnp.float32),
        "cls_b": noise(key_list[18], (LAYERS, CLASSES), 0.5, 3.0, (), jnp.float32),
    }


@jax.custom_vjp
def low(v):
    return lax.optimization_barrier(v.astype(jnp.bfloat16)).astype(jnp.float32)

@jax.custom_vjp
def low_back(v):
    return v

def low_keep(v):
    return (low(v), None)

def low_pass(kept, grad):
    return (grad,)

def back_keep(v):
    return (v, None)

def back_low(kept, grad):
    return (low(grad),)
low.defvjp(low_keep, low_pass)
low_back.defvjp(back_keep, back_low)
epsilon = 1e-12
highest = lax.Precision.HIGHEST

def matmul(left, right):
    return jnp.dot(left, right, precision=highest, preferred_element_type=jnp.float32)

def layer_norm(values, gain, shift):
    row_mean = lax.optimization_barrier(jnp.mean(values, axis=1, keepdims=True))
    centered = values - row_mean
    variance = lax.optimization_barrier(jnp.mean(centered * centered, axis=1, keepdims=True))
    return centered * lax.rsqrt(variance + epsilon) * gain + shift

def layout(length_row):
    ends = jnp.cumsum(length_row, dtype=jnp.int32)
    positions = jnp.arange(TOK_MB, dtype=jnp.int32)
    segment = lax.optimization_barrier(jnp.sum((positions[:, None] >= ends[None, :-1]).astype(jnp.int32), axis=1))
    return (segment, ends - length_row, (length_row > 0).astype(jnp.float32))

def block(x_res, x_low, layer_params, segment):
    w_qkv, b_qv, w_out, b_out, w_in, b_in, w_down, b_down, norm_gains, norm_shifts = layer_params
    same_seq = (segment[:, None] == segment[None, :])[None]
    group_width = D // GROUPS
    hidden_width = FF // GROUPS
    head_count = group_width // HEAD
    attn_total = jnp.zeros((TOK_MB, D), jnp.float32)
    for group_index in range(GROUPS):
        columns = slice(group_index * group_width, (group_index + 1) * group_width)
        x_part = low_back(x_low)
        queries = low_back(low(matmul(x_part, w_qkv[0][:, columns]) + b_qv[0][columns]))
        keys_low = low_back(low(matmul(x_part, w_qkv[1][:, columns])))
        values_low = low_back(low(matmul(x_part, w_qkv[2][:, columns]) + b_qv[1][columns]))
        query_heads = queries.reshape(TOK_MB, head_count, HEAD)
        key_heads = keys_low.reshape(TOK_MB, head_count, HEAD)
        value_heads = values_low.reshape(TOK_MB, head_count, HEAD)
        scores = low_back(jnp.einsum('qhd,khd->hqk', query_heads, key_heads, precision=highest) * HEAD ** (-0.5))
        probs = jax.nn.softmax(jnp.where(same_seq, scores, -1e+30), axis=2)
        mixed = jnp.einsum('hqk,khd->qhd', low(probs), value_heads, precision=highest).reshape(TOK_MB, group_width)
        mixed = low_back(low(mixed))
        attn_total = attn_total + low(matmul(mixed, w_out[columns, :]))
    attn_out = low_back(attn_total)
    hidden = layer_norm(attn_out + b_out + x_res, norm_gains[0], norm_shifts[0])
    hidden_low = low(hidden)
    ffn_total = jnp.zeros((TOK_MB, D), jnp.float32)
    for group_index in range(GROUPS):
        columns = slice(group_index * hidden_width, (group_index + 1) * hidden_width)
        hidden_part = low_back(hidden_low)
        pre_act = low_back(matmul(hidden_part, w_in[:, columns]) + b_in[columns])
        act_low = low(jax.nn.gelu(pre_act, approximate=False))
        ffn_total = ffn_total + low(matmul(act_low, w_down[columns, :]))
    ffn_out = low_back(ffn_total)
    return layer_norm(ffn_out + b_down + hidden, norm_gains[1], norm_shifts[1])

def reference(tokens, cotangent, packing, lengths, labels, w_qkv, b_qv, w_out, b_out, w_in, b_in, w_down, b_down, norm_gains, norm_shifts, pool_w, pool_b, cls_w, cls_b):
    params = tuple((weight.astype(jnp.float32) for weight in (w_qkv, b_qv, w_out, b_out, w_in, b_in, w_down, b_down, norm_gains, norm_shifts, pool_w, pool_b, cls_w, cls_b)))
    packed_x = jnp.zeros((TOKENS, D), jnp.float32).at[packing].set(tokens.astype(jnp.float32))
    packed_cot = jnp.zeros((TOKENS, D), jnp.float32).at[packing].set(cotangent.astype(jnp.float32))
    batch_x = packed_x.reshape(BATCHES, TOK_MB, D)
    batch_cot = packed_cot.reshape(BATCHES, TOK_MB, D)
    label_rows = labels.reshape(BATCHES, SLOTS)

    def forward(weights, inputs, length_row, label_row):
        segment, starts, valid = layout(length_row)
        picks = jnp.minimum(starts, TOK_MB - 1)
        onehot = (label_row[:, None] == jnp.arange(CLASSES, dtype=jnp.int32)[None, :]).astype(jnp.float32)
        x_res = inputs
        x_low = low(inputs)
        exit_list = []
        loss = jnp.zeros((), jnp.float32)
        for layer_index in range(LAYERS):
            layer_params = tuple((weight[layer_index] for weight in weights[:10]))
            output = block(x_res, x_low, layer_params, segment)
            out_low = low(output)
            pooled = jnp.tanh(matmul(out_low[picks], weights[10][layer_index]) + weights[11][layer_index])
            logits = (matmul(pooled, weights[12][layer_index]) + weights[13][layer_index]) * valid[:, None]
            loss = loss + jnp.sum(valid * (jax.nn.logsumexp(logits, axis=1) - lax.optimization_barrier(jnp.sum(logits * onehot, axis=1))))
            exit_list.append(logits)
            x_res = output
            x_low = out_low
        return (x_low, jnp.stack(exit_list), loss)

    def step(totals, items):
        inputs, cot_rows, length_row, label_row = items

        def apply(weights, values):
            return forward(weights, values, length_row, label_row)
        results, pullback = jax.vjp(apply, params, inputs)
        weight_grads, input_grad = pullback((cot_rows, jnp.zeros_like(results[1]), jnp.ones_like(results[2])))
        totals = tuple((total + grad for total, grad in zip(totals, weight_grads)))
        return (totals, (results[0], results[1], input_grad))
    zero_grads = tuple((jnp.zeros_like(weight) for weight in params))
    totals, (outputs, exit_rows, input_grads) = lax.scan(step, zero_grads, (batch_x, batch_cot, lengths, label_rows))
    block_out = outputs.reshape(TOKENS, D)[packing].astype(jnp.bfloat16)
    tokens_grad = input_grads.reshape(TOKENS, D)[packing].astype(jnp.bfloat16)
    exits = jnp.transpose(exit_rows, (1, 0, 2, 3)).reshape(LAYERS, NSEQ, CLASSES)
    return (block_out, exits, tokens_grad, totals[0], totals[1], totals[2], totals[3], totals[4], totals[5], totals[6], totals[7], totals[8], totals[9], totals[10], totals[11], totals[12], totals[13])
```

```python
import functools
import math

import jax
import jax.numpy as jnp
from jax import lax
from jax.experimental import pallas as pl
from jax.experimental.pallas import tpu as pltpu
from jax.sharding import PartitionSpec as P

HEAD = 64
PAIR = 2 * HEAD
STEP = 16

epsilon = 1e-12
highest = lax.Precision.HIGHEST
root_half = 1.0 / math.sqrt(2.0)
inv_root_tau = 1.0 / math.sqrt(2.0 * math.pi)
f32 = jnp.float32
bf16 = jnp.bfloat16

TREE = (2, 6, 3, 7, 0, 4, 1, 5, 9, 13, 11, 15, 8, 12, 10, 14)


def dot(left, right):
    return lax.dot_general(left, right, (((1,), (0,)), ((), ())), preferred_element_type=f32)


def dot_cols(left, right):
    return lax.dot_general(left, right, (((1,), (1,)), ((), ())), preferred_element_type=f32)


def dot_rows(left, right):
    return lax.dot_general(left, right, (((0,), (0,)), ((), ())), preferred_element_type=f32)


def over_rows(count, fn, step=STEP):
    def one(index, carry):
        fn(pl.ds(pl.multiple_of(index * step, step), step))
        return carry

    lax.fori_loop(0, count // step, one, 0)


def norm_rows(values):
    centered = values - jnp.mean(values, axis=1, keepdims=True)
    scaling = lax.rsqrt(jnp.mean(centered * centered, axis=1, keepdims=True) + epsilon)
    return centered * scaling, scaling


def norm_grad(grad, gain, normed, scaling):
    scaled = grad * gain
    mean_grad = jnp.mean(scaled, axis=1, keepdims=True)
    mean_dot = jnp.mean(scaled * normed, axis=1, keepdims=True)
    return scaling * (scaled - mean_grad - normed * mean_dot)


def fetch(pieces, held, sems):
    copies = []
    start = 0
    for index, piece in enumerate(pieces):
        rows = piece.shape[0]
        copies.append(
            pltpu.make_async_copy(piece, held.at[pl.ds(start, rows), :], sems.at[index])
        )
        start += rows
    for copy in copies:
        copy.start()
    return copies


def finish(copies):
    for copy in copies:
        copy.wait()


def same_segment(ends, batch, rows):
    at_row = lax.broadcasted_iota(jnp.int32, (rows, rows), 0)
    at_col = lax.broadcasted_iota(jnp.int32, (rows, rows), 1)
    seg_row = jnp.zeros((rows, rows), jnp.int32)
    seg_col = jnp.zeros((rows, rows), jnp.int32)
    for slot in range(ends.shape[1] - 1):
        seg_row = seg_row + (at_row >= ends[batch, slot]).astype(jnp.int32)
        seg_col = seg_col + (at_col >= ends[batch, slot]).astype(jnp.int32)
    return seg_row == seg_col


def attention_kernel(*refs, first, count):
    refs = list(refs)
    if first:
        x_in = refs.pop(0)
    else:
        own, other, hidden, vec = refs[:4]
        refs = refs[4:]
    pieces, refs = refs[:count], refs[count:]
    bias, ends = refs[:2]
    refs = refs[2:]
    if first:
        x_low = x_in
    else:
        x_low, x_res = refs[:2]
        refs = refs[2:]
    qkv, probs, mixed, part, held, sems = refs
    copies = fetch(pieces, held, sems)
    total, width = part.shape
    group = mixed.shape[1]
    if not first:

        def norm(rows):
            values = (
                own[rows, :].astype(f32) + other[rows, :].astype(f32) + vec[0:1, :] + hidden[rows, :]
            )
            result = norm_rows(values)[0] * vec[1:2, :] + vec[2:3, :]
            x_res[rows, :] = result
            x_low[rows, :] = result.astype(bf16)

        over_rows(total, norm)
    finish(copies)
    for index in range(3):
        cols = slice(index * group, (index + 1) * group)
        values = dot(x_low[...], held[:, cols])
        if index != 1:
            values = values + bias[index // 2 : index // 2 + 1, :]
        qkv[:, cols] = values.astype(bf16)
    batches = ends.shape[0]
    rows = total // batches
    low_half = lax.broadcasted_iota(jnp.int32, (rows, PAIR), 1) < HEAD
    zero = jnp.zeros((rows, PAIR), bf16)
    for batch in range(batches):
        keep = same_segment(ends, batch, rows)
        span = slice(batch * rows, (batch + 1) * rows)
        for pair in range(group // PAIR):
            query = qkv[span, pair * PAIR : (pair + 1) * PAIR]
            key = qkv[span, group + pair * PAIR : group + (pair + 1) * PAIR]
            value = qkv[span, 2 * group + pair * PAIR : 2 * group + (pair + 1) * PAIR]
            halves = []
            for side in range(2):
                masked = jnp.where(low_half if side == 0 else ~low_half, query, zero)
                scores = dot_cols(masked, key) * HEAD ** (-0.5)
                scores = jnp.where(keep, scores, -1e30)
                weights = jnp.exp(scores - jnp.max(scores, axis=1, keepdims=True))
                prob = weights / jnp.sum(weights, axis=1, keepdims=True)
                head = (batch * (group // PAIR) + pair) * 2 + side
                probs[head * rows : (head + 1) * rows, :] = prob
                halves.append(dot(prob.astype(bf16), value))
            mixed[span, pair * PAIR : (pair + 1) * PAIR] = jnp.where(
                low_half, halves[0], halves[1]
            ).astype(bf16)
    part[...] = dot_cols(mixed[...], held[:, 3 * group : 4 * group]).astype(bf16)


def ffn_kernel(*refs, count):
    refs = list(refs)
    own, other, x_res, vec = refs[:4]
    refs = refs[4:]
    in_pieces, down_pieces, refs = refs[:count], refs[count : 2 * count], refs[2 * count :]
    bias, hidden, normed, scale, hidden_low, pre_act, act_low, part = refs[:8]
    held_in, held_down, in_sems, down_sems = refs[8:]
    in_copies = fetch(in_pieces, held_in, in_sems)
    down_copies = fetch(down_pieces, held_down, down_sems)
    total = part.shape[0]

    def norm(rows):
        values = (
            own[rows, :].astype(f32)
            + other[rows, :].astype(f32)
            + vec[0:1, :]
            + x_res[rows, :].astype(f32)
        )
        unit, scaling = norm_rows(values)
        result = unit * vec[1:2, :] + vec[2:3, :]
        normed[rows, :] = unit
        scale[rows, :] = scaling
        hidden[rows, :] = result
        hidden_low[rows, :] = result.astype(bf16)

    over_rows(total, norm)
    finish(in_copies)
    pre_act[...] = dot(hidden_low[...], held_in[...]) + bias[...]

    def act(rows):
        values = pre_act[rows, :]
        act_low[rows, :] = (values * (0.5 * (1.0 + lax.erf(values * root_half)))).astype(bf16)

    over_rows(total, act)
    finish(down_copies)
    part[...] = dot_cols(act_low[...], held_down[...]).astype(bf16)


def split_rows(values, outs):
    start = 0
    for out in outs:
        rows = out.shape[0]
        out[...] = values[start : start + rows, :].astype(bf16)
        start += rows


def grads_of(left, right, outs):
    start = 0
    for out in outs:
        rows = out.shape[0]
        out[...] = dot_rows(left[:, start : start + rows], right).astype(bf16)
        start += rows


def exit_kernel(*refs, last, count, classes):
    refs = list(refs)
    own, other, hidden, vec = refs[:4]
    refs = refs[4:]
    if last:
        cot = refs.pop(0)
    else:
        x_own, x_other, x_direct = refs[:3]
        refs = refs[3:]
    pool_pieces, far_pieces, refs = refs[:count], refs[count : 2 * count], refs[2 * count :]
    pool_b, cls_t, cls_b, aux, act_low = refs[:5]
    refs = refs[5:]
    exits, g_c, g_ffn, sums = refs[:4]
    down_outs, pool_outs, refs = refs[4:8], refs[8:12], refs[12:]
    if last:
        out_low = refs.pop(0)
    held, far, near_sems, far_sems, normed, scale = refs[:6]
    if not last:
        out_low = refs[6]
    grad_out = refs[-1]
    near_copies = fetch(pool_pieces, held, near_sems)
    far_copies = fetch(far_pieces, far, far_sems)
    total, width = g_c.shape
    half = held.shape[1]

    def norm(rows):
        values = (
            own[rows, :].astype(f32) + other[rows, :].astype(f32) + vec[0:1, :] + hidden[rows, :]
        )
        unit, scaling = norm_rows(values)
        normed[rows, :] = unit
        scale[rows, :] = scaling
        out_low[rows, :] = (unit * vec[1:2, :] + vec[2:3, :]).astype(bf16)

    over_rows(total, norm)
    slots = aux.shape[0]
    picks = aux[:, 0:1].astype(jnp.int32)
    valid = aux[:, 1:2]
    chosen = (lax.broadcasted_iota(jnp.int32, (slots, total), 1) == picks).astype(bf16)
    taken = dot(chosen, out_low[...]).astype(bf16)
    finish(near_copies)
    finish(far_copies)
    pooled = jnp.tanh(
        jnp.concatenate([dot(taken, held[...]), dot(taken, far[...])], axis=1) + pool_b[...]
    )
    logits = [
        (jnp.sum(pooled * cls_t[index : index + 1, :], axis=1, keepdims=True)
         + cls_b[0:1, index : index + 1]) * valid
        for index in range(classes)
    ]
    top = functools.reduce(jnp.maximum, logits)
    powers = [jnp.exp(item - top) for item in logits]
    norm_sum = sum(powers[1:], powers[0])
    lane = lax.broadcasted_iota(jnp.int32, exits.shape, 1)
    shown = jnp.zeros(exits.shape, f32)
    grads = []
    for index in range(classes):
        shown = jnp.where(lane == index, logits[index], shown)
        grads.append((powers[index] / norm_sum - aux[:, 2 + index : 3 + index]) * valid)
    exits[...] = shown
    back = grads[0] * cls_t[0:1, :]
    for index in range(1, classes):
        back = back + grads[index] * cls_t[index : index + 1, :]
    grad_z = back * (1.0 - pooled * pooled)
    high = grad_z.astype(bf16)
    rest = (grad_z - high.astype(f32)).astype(bf16)
    both = jnp.concatenate([high, rest], axis=0)
    twice = jnp.concatenate([taken, taken], axis=0)
    split_rows(dot_rows(twice, both[:, :half]), pool_outs)
    pick = dot_cols(both[:, :half], held[...]) + dot_cols(both[:, half:], far[...])
    pick = pick[:slots, :] + pick[slots:, :]
    pick_high = pick.astype(bf16)
    pick_rest = (pick - pick_high.astype(f32)).astype(bf16)
    twice_chosen = jnp.concatenate([chosen, chosen], axis=0)
    grad_out[...] = dot_rows(twice_chosen, jnp.concatenate([pick_high, pick_rest], axis=0))
    sums[...] = jnp.zeros(sums.shape, f32)

    def back_norm(rows):
        if last:
            grad = cot[rows, :].astype(f32)
        else:
            grad = x_own[rows, :].astype(f32) + x_other[rows, :].astype(f32) + x_direct[rows, :]
        grad = grad + grad_out[rows, :]
        unit = normed[rows, :]
        result = norm_grad(grad, vec[1:2, :], unit, scale[rows, :])
        g_c[rows, :] = result
        g_ffn[rows, :] = result.astype(bf16)
        sums[0:1, :] += jnp.sum(result, axis=0, keepdims=True)
        sums[1:2, :] += jnp.sum(grad * unit, axis=0, keepdims=True)
        sums[2:3, :] += jnp.sum(grad, axis=0, keepdims=True)

    over_rows(total, back_norm)
    sums[3:4, :] = jnp.sum(grad_z, axis=0, keepdims=True)
    spot = lax.broadcasted_iota(jnp.int32, (1, width), 1)
    tail = jnp.zeros((1, width), f32)
    for index in range(classes):
        sums[5 + index : 6 + index, :] = jnp.sum(grads[index] * pooled, axis=0, keepdims=True)
        tail = jnp.where(spot == index, jnp.sum(grads[index], axis=0, keepdims=True), tail)
    sums[4:5, :] = tail
    grads_of(g_ffn, act_low[...], down_outs)


def ffn_back_kernel(*refs, count):
    refs = list(refs)
    g_ffn, pre_act, hidden_low = refs[:3]
    refs = refs[3:]
    in_pieces, down_pieces, refs = refs[:count], refs[count : 2 * count], refs[2 * count :]
    sums, part = refs[:2]
    in_outs, refs = refs[2:6], refs[6:]
    held_in, held_down, in_sems, down_sems, g_act, g_pre = refs
    down_copies = fetch(down_pieces, held_down, down_sems)
    in_copies = fetch(in_pieces, held_in, in_sems)
    total = part.shape[0]
    finish(down_copies)
    g_act[...] = dot(g_ffn[...], held_down[...])
    sums[...] = jnp.zeros(sums.shape, f32)

    def slope(rows):
        values = pre_act[rows, :]
        cdf = 0.5 * (1.0 + lax.erf(values * root_half))
        pdf = jnp.exp(-0.5 * values * values) * inv_root_tau
        result = (g_act[rows, :] * (cdf + values * pdf)).astype(bf16)
        g_pre[rows, :] = result
        sums[0:1, :] += jnp.sum(result.astype(f32), axis=0, keepdims=True)

    over_rows(total, slope)
    grads_of(hidden_low, g_pre[...], in_outs)
    finish(in_copies)
    part[...] = dot_cols(g_pre[...], held_in[...]).astype(bf16)


def attention_back_kernel(*refs, count):
    refs = list(refs)
    g_c, own, other, normed, scale, vec = refs[:6]
    refs = refs[6:]
    pieces, refs = refs[:count], refs[count:]
    qkv, probs, mixed, x_low = refs[:4]
    refs = refs[4:]
    g_a, part, sums, bias_sums = refs[:4]
    outs, refs = refs[4:8], refs[8:]
    held, sems, g_attn, g_mixed, g_qkv = refs
    copies = fetch(pieces, held, sems)
    total, width = g_c.shape
    group = mixed.shape[1]
    sums[...] = jnp.zeros(sums.shape, f32)

    def back_norm(rows):
        grad = g_c[rows, :] + (own[rows, :].astype(f32) + other[rows, :].astype(f32))
        unit = normed[rows, :]
        result = norm_grad(grad, vec[1:2, :], unit, scale[rows, :])
        g_a[rows, :] = result
        g_attn[rows, :] = result.astype(bf16)
        sums[0:1, :] += jnp.sum(result, axis=0, keepdims=True)
        sums[1:2, :] += jnp.sum(grad * unit, axis=0, keepdims=True)
        sums[2:3, :] += jnp.sum(grad, axis=0, keepdims=True)

    over_rows(total, back_norm)
    finish(copies)
    g_mixed[...] = dot(g_attn[...], held[:, 3 * group : 4 * group]).astype(bf16)
    rows = probs.shape[1]
    batches = total // rows
    low_half = lax.broadcasted_iota(jnp.int32, (rows, PAIR), 1) < HEAD
    zero = jnp.zeros((rows, PAIR), bf16)
    factor = HEAD ** (-0.5)
    for batch in range(batches):
        span = slice(batch * rows, (batch + 1) * rows)
        for pair in range(group // PAIR):
            cols = slice(pair * PAIR, (pair + 1) * PAIR)
            key_cols = slice(group + pair * PAIR, group + (pair + 1) * PAIR)
            value_cols = slice(2 * group + pair * PAIR, 2 * group + (pair + 1) * PAIR)
            query, key, value = qkv[span, cols], qkv[span, key_cols], qkv[span, value_cols]
            grad = g_mixed[span, cols]
            sides = []
            for side in range(2):
                head = (batch * (group // PAIR) + pair) * 2 + side
                prob = probs[head * rows : (head + 1) * rows, :]
                masked = jnp.where(low_half if side == 0 else ~low_half, grad, zero)
                grad_prob = dot_cols(masked, value)
                row_dot = jnp.sum(prob * grad_prob, axis=1, keepdims=True)
                grad_score = (prob * (grad_prob - row_dot)).astype(bf16)
                sides.append(
                    (
                        dot(grad_score, key) * factor,
                        dot_rows(grad_score, query) * factor,
                        dot_rows(prob.astype(bf16), grad),
                    )
                )
            for where_to, near, far in zip((cols, key_cols, value_cols), sides[0], sides[1]):
                g_qkv[span, where_to] = jnp.where(low_half, near, far).astype(bf16)
    part[...] = dot_cols(g_qkv[...], held[:, : 3 * group]).astype(bf16)
    bias_sums[:, :group] = jnp.sum(g_qkv[:, :group].astype(f32), axis=0, keepdims=True)
    bias_sums[:, group:] = jnp.sum(g_qkv[:, 2 * group :].astype(f32), axis=0, keepdims=True)
    start = 0
    for out in outs:
        out_rows = out.shape[0]
        block = slice(start, start + out_rows)
        out[:, : 3 * group] = dot_rows(x_low[:, block], g_qkv[...]).astype(bf16)
        out[:, 3 * group :] = dot_rows(g_attn[:, block], mixed[...]).astype(bf16)
        start += out_rows


VM = pltpu.VMEM
SM = pltpu.SMEM
ANY = pl.ANY


def launch(kernel, name, ins, outs, scratch):
    specs = [pl.BlockSpec(memory_space=space) for _, space in ins]
    return pl.pallas_call(
        kernel,
        name=name,
        in_specs=specs,
        out_shape=[jax.ShapeDtypeStruct(shape, kind) for shape, kind in outs],
        out_specs=[pl.BlockSpec(memory_space=VM) for _ in outs],
        scratch_shapes=scratch,
    )(*[item for item, _ in ins])


def vm(*items):
    return [(item, VM) for item in items]


def anywhere(items):
    return [(item, ANY) for item in items]


def hop(value, flip, size):
    return lax.ppermute(value, "dp", [(index, index ^ flip) for index in range(size)])


def across(value):
    return lax.ppermute(value, "tensor", [(0, 1), (1, 0)])


def gather_tree(shard, size):
    near = [hop(shard, 4 * step, size) for step in (1, 2, 3)]
    half_a = jnp.concatenate([shard, near[0]], axis=0)
    half_b = jnp.concatenate([near[1], near[2]], axis=0)
    a_x = hop(half_a, 1, size)
    b_y = hop(half_b, 2, size)
    a_y = hop(half_a, 2, size)
    b_x = hop(half_b, 1, size)
    a_xy = hop(a_x, 2, size)
    b_xy = hop(b_y, 1, size)
    return [a_y, a_xy, half_a, a_x, b_x, b_xy, half_b, b_y]


def reduce_tree(parts, size):
    send_a, keep_a, send_b, keep_b = parts
    rows = keep_a.shape[0] // 2
    unit = rows // 2
    got_a = hop(send_a, 2, size)
    got_b = hop(send_b, 1, size)
    next_a = (keep_a[rows:].astype(f32) + got_a[rows:].astype(f32)).astype(bf16)
    next_b = (keep_b[rows:].astype(f32) + got_b[rows:].astype(f32)).astype(bf16)
    far_a = hop(next_a, 1, size)
    far_b = hop(next_b, 2, size)
    sum_a = keep_a[:rows].astype(f32) + got_a[:rows].astype(f32) + far_a.astype(f32)
    sum_b = keep_b[:rows].astype(f32) + got_b[:rows].astype(f32) + far_b.astype(f32)
    z_one = hop(sum_a[unit:].astype(bf16), 4, size)
    z_two = hop(sum_b[:unit].astype(bf16), 8, size)
    z_three = hop(sum_b[unit:].astype(bf16), 12, size)
    return sum_a[:unit] + z_one.astype(f32) + z_two.astype(f32) + z_three.astype(f32)


def onehot(values, count):
    return (jnp.arange(count, dtype=jnp.int32)[:, None] == values[None, :]).astype(bf16)


def move(left, right, rows=False):
    return (dot_rows if rows else dot)(left, right).astype(bf16)


def exact(left, right):
    return jnp.dot(left, right, precision=highest, preferred_element_type=f32)


def body(
    tokens,
    cotangent,
    packing,
    lengths,
    labels,
    w_qkv,
    b_qv,
    w_out,
    b_out,
    w_in,
    b_in,
    w_down,
    b_down,
    norm_gains,
    norm_shifts,
    pool_w,
    pool_b,
    cls_w,
    cls_b,
):
    total, width = tokens.shape
    micro, slots = lengths.shape
    row_count = total // micro
    layers = w_qkv.shape[0]
    classes = cls_w.shape[2]
    group = b_qv.shape[2]
    ff = b_in.shape[1]
    size = lax.axis_size("dp")
    data_index = lax.axis_index("dp")
    tensor_index = lax.axis_index("tensor")
    share = total // size
    half = width // 2
    tree = size == 16 and width % 256 == 0

    def gather(shard):
        if tree:
            return gather_tree(shard, size)
        return [lax.all_gather(shard, "dp", axis=0, tiled=True)]

    def halves(value):
        return lax.dynamic_slice_in_dim(value, tensor_index * half, half, axis=value.ndim - 1)

    attn_w, in_w, down_w, pool_near = [], [], [], []
    for layer in range(layers):
        attn_w.append(
            gather(jnp.concatenate([w_qkv[layer, 0], w_qkv[layer, 1], w_qkv[layer, 2], w_out[layer].T], axis=1))
        )
        in_w.append(gather(w_in[layer]))
        if layer == layers - 1:
            pool_near = [gather(halves(pool_w[item])) for item in range(layers)]
        down_w.append(gather(w_down[layer].T))
    pool_far = [[across(piece) for piece in pieces] for pieces in pool_near]
    count = len(attn_w[0])

    column = jnp.arange(width, dtype=jnp.int32)
    if tree:
        unit = width // size
        order = jnp.asarray(TREE, jnp.int32) ^ data_index
        natural = jnp.repeat(order, unit) * unit + column % unit
    else:
        natural = column
    shuffle = onehot(natural, width)
    shuffle_half = halves(shuffle.T)

    own_places = lax.dynamic_slice_in_dim(packing, data_index * total, total)
    own_targets = own_places // total
    index = jnp.arange(total, dtype=jnp.int32)
    earlier = (own_targets[:, None] == own_targets[None, :]) & (index[None, :] < index[:, None])
    slot = own_targets * share + jnp.sum(earlier.astype(jnp.int32), axis=1)
    send = onehot(slot, total)
    table = packing.reshape(size, total)
    mine = table // total == data_index
    before = (index[:, None] < index[None, :]).astype(bf16)
    rank = dot(mine.astype(bf16), before).astype(jnp.int32)
    hit = mine[:, None, :] & (rank[:, None, :] == jnp.arange(share, dtype=jnp.int32)[None, :, None])
    places = jnp.sum(jnp.where(hit, (table - data_index * total)[:, None, :], 0), axis=2)
    place = onehot(places.reshape(total), total)

    def swap(value):
        return lax.all_to_all(value, "dp", split_axis=0, concat_axis=0, tiled=True)

    def joined(value):
        far = across(value)
        return jnp.where(
            tensor_index == 0,
            jnp.concatenate([value, far], axis=1),
            jnp.concatenate([far, value], axis=1),
        )

    loaded = jnp.concatenate([halves(tokens), halves(cotangent)], axis=1)
    arrived = move(place, swap(move(send, loaded)))
    far = across(arrived)
    first = jnp.where(tensor_index == 0, arrived, far)
    second = jnp.where(tensor_index == 0, far, arrived)
    packed_tokens = move(jnp.concatenate([first[:, :half], second[:, :half]], axis=1), shuffle)
    packed_cot = move(jnp.concatenate([first[:, half:], second[:, half:]], axis=1), shuffle)

    def unpack(value):
        back = swap(move(place, move(value, shuffle_half), rows=True))
        return joined(move(send, back, rows=True))

    vectors = exact(
        jnp.concatenate(
            [b_out, b_down, norm_gains.reshape(2 * layers, width), norm_shifts.reshape(2 * layers, width)]
        ),
        shuffle.astype(f32),
    )

    def vector_rows(layer, which):
        base = [layer + (0 if which == 0 else layers), 2 * layers + 2 * layer + which, 4 * layers + 2 * layer + which]
        return jnp.concatenate([vectors[item : item + 1] for item in base])

    def own_first(value):
        return jnp.where(tensor_index == 0, value, jnp.roll(value, half, axis=-1))

    ends = jnp.cumsum(lengths, axis=1, dtype=jnp.int32)
    starts = ends - lengths
    picks = jnp.minimum(starts, row_count - 1) + row_count * jnp.arange(micro, dtype=jnp.int32)[:, None]
    label_hot = (labels[:, None] == jnp.arange(classes, dtype=jnp.int32)[None, :]).astype(f32)
    aux = jnp.concatenate(
        [
            picks.reshape(micro * slots, 1).astype(f32),
            (lengths > 0).astype(f32).reshape(micro * slots, 1),
            label_hot,
            jnp.zeros((micro * slots, 126 - classes), f32),
        ],
        axis=1,
    )

    sem = pltpu.SemaphoreType.DMA((count,))
    heads = group // HEAD
    saved = []
    x_res = packed_tokens
    x_low = packed_tokens
    incoming = None
    for layer in range(layers):
        is_first = layer == 0
        outs = [
            ((total, 3 * group), bf16),
            ((micro * heads * row_count, row_count), f32),
            ((total, group), bf16),
            ((total, width), bf16),
        ]
        if is_first:
            ins = vm(packed_tokens)
        else:
            outs = [((total, width), bf16), ((total, width), f32)] + outs
            ins = vm(*incoming)
        result = launch(
            functools.partial(attention_kernel, first=is_first, count=count),
            "attention",
            ins + anywhere(attn_w[layer]) + vm(b_qv[layer]) + [(ends, SM)],
            outs,
            [VM((width, 4 * group), bf16), sem],
        )
        if not is_first:
            x_low, x_res = result[:2]
            result = result[2:]
        qkv, probs, mixed, attn_part = result
        hidden, normed, scale, hidden_low, pre_act, act_low, ffn_part = launch(
            functools.partial(ffn_kernel, count=count),
            "ffn",
            vm(attn_part, across(attn_part), x_res, vector_rows(layer, 0))
            + anywhere(in_w[layer])
            + anywhere(down_w[layer])
            + vm(b_in[layer][None]),
            [
                ((total, width), f32),
                ((total, width), f32),
                ((total, 1), f32),
                ((total, width), bf16),
                ((total, ff), f32),
                ((total, ff), bf16),
                ((total, width), bf16),
            ],
            [VM((width, ff), bf16), VM((width, ff), bf16), sem, sem],
        )
        incoming = (ffn_part, across(ffn_part), hidden, vector_rows(layer, 1))
        saved.append((x_low, qkv, probs, mixed, normed, scale, hidden_low, pre_act, act_low, incoming))

    quarter = width // 4
    exit_list = [None] * layers
    sums_list = [None] * layers
    chunks = [None] * layers
    block_out = None
    passed = None
    for layer in reversed(range(layers)):
        x_low, qkv, probs, mixed, normed, scale, hidden_low, pre_act, act_low, incoming = saved[layer]
        is_last = layer == layers - 1
        outs = [
            ((micro * slots, 128), f32),
            ((total, width), f32),
            ((total, width), bf16),
            ((8, width), f32),
        ]
        outs += [((quarter, ff), bf16)] * 4 + [((quarter, half), bf16)] * 4
        scratch = [VM((width, half), bf16), VM((width, half), bf16), sem, sem, VM((total, width), f32), VM((total, 1), f32)]
        if is_last:
            outs.append(((total, width), bf16))
        else:
            scratch.append(VM((total, width), bf16))
        scratch.append(VM((total, width), f32))
        result = launch(
            functools.partial(exit_kernel, last=is_last, count=count, classes=classes),
            "exit",
            vm(*incoming)
            + vm(*((packed_cot,) if is_last else passed))
            + anywhere(pool_near[layer])
            + anywhere(pool_far[layer])
            + vm(own_first(pool_b[layer])[None], own_first(cls_w[layer].T), cls_b[layer][None], aux, act_low),
            outs,
            scratch,
        )
        exits, g_c, g_ffn, exit_sums = result[:4]
        down_parts, pool_parts = result[4:8], result[8:12]
        if is_last:
            block_out = unpack(result[12])
        back = launch(
            functools.partial(ffn_back_kernel, count=count),
            "ffn_back",
            vm(g_ffn, pre_act, hidden_low) + anywhere(in_w[layer]) + anywhere(down_w[layer]),
            [((1, ff), f32), ((total, width), bf16)] + [((quarter, ff), bf16)] * 4,
            [
                VM((width, ff), bf16),
                VM((width, ff), bf16),
                sem,
                sem,
                VM((total, ff), f32),
                VM((total, ff), bf16),
            ],
        )
        in_sums, hidden_part = back[:2]
        in_parts = back[2:]
        back = launch(
            functools.partial(attention_back_kernel, count=count),
            "attention_back",
            vm(g_c, hidden_part, across(hidden_part), normed, scale, vector_rows(layer, 0))
            + anywhere(attn_w[layer])
            + vm(qkv, probs, mixed, x_low),
            [((total, width), f32), ((total, width), bf16), ((8, width), f32), ((1, 2 * group), f32)]
            + [((quarter, 4 * group), bf16)] * 4,
            [
                VM((width, 4 * group), bf16),
                sem,
                VM((total, width), bf16),
                VM((total, group), bf16),
                VM((total, 3 * group), bf16),
            ],
        )
        g_a, x_part, attn_sums, bias_sums = back[:4]
        attn_parts = back[4:]
        passed = (x_part, across(x_part), g_a)
        exit_list[layer] = exits
        sums_list[layer] = (exit_sums, in_sums, attn_sums, bias_sums)
        chunks[layer] = (down_parts, pool_parts, in_parts, attn_parts)
    final = (passed[0].astype(f32) + passed[1].astype(f32) + passed[2]).astype(bf16)
    tokens_grad = unpack(final)

    def reduce_rows(parts):
        if tree:
            return reduce_tree(parts, size)
        return lax.psum_scatter(
            jnp.concatenate(parts, axis=0), "dp", scatter_dimension=0, tiled=True
        ).astype(f32)

    grads = [[reduce_rows(parts) for parts in chunks[layer]] for layer in range(layers)]
    qkv_grad = jnp.stack(
        [
            jnp.stack([grads[layer][3][:, item * group : (item + 1) * group] for item in range(3)])
            for layer in range(layers)
        ]
    )
    out_grad = jnp.stack([grads[layer][3][:, 3 * group :].T for layer in range(layers)])
    in_grad = jnp.stack([grads[layer][2] for layer in range(layers)])
    down_grad = jnp.stack([grads[layer][0].T for layer in range(layers)])
    pool_grad = joined(jnp.concatenate([grads[layer][1] for layer in range(layers)], axis=0))
    pool_grad = pool_grad.reshape(layers, pool_w.shape[1], width)

    ordered, plain = [], []
    for layer in range(layers):
        exit_sums, in_sums, attn_sums, bias_sums = sums_list[layer]
        ordered += [exit_sums[:3], attn_sums[:3]]
        plain += [exit_sums[3:], in_sums.reshape(ff // width, width), bias_sums]
    ordered = lax.dot_general(
        jnp.concatenate(ordered),
        shuffle.astype(f32),
        (((1,), (1,)), ((), ())),
        precision=highest,
        preferred_element_type=f32,
    )
    vector_sum = jnp.concatenate([ordered] + plain)
    if tree:
        for flip in (1, 2, 4, 8):
            vector_sum = vector_sum + hop(vector_sum, flip, size)
    else:
        vector_sum = lax.psum(vector_sum, "dp")
    ordered, plain = vector_sum[: 6 * layers], vector_sum[6 * layers :]
    each = plain.shape[0] // layers
    plain = plain.reshape(layers, each, width)
    ordered = ordered.reshape(layers, 6, width)
    natural_exit = own_first(plain[:, :5])
    cls_sums = plain[:, 1, :classes]
    cls_rows = natural_exit[:, 2 : 2 + classes]
    in_rows = plain[:, 5 : 5 + ff // width].reshape(layers, ff)
    bias_rows = plain[:, 5 + ff // width].reshape(layers, 2, group)
    return (
        block_out,
        jnp.stack(exit_list)[:, :, :classes],
        tokens_grad,
        qkv_grad,
        bias_rows,
        out_grad,
        ordered[:, 3],
        in_grad,
        in_rows,
        down_grad,
        ordered[:, 0],
        jnp.stack([ordered[:, 4], ordered[:, 1]], axis=1),
        jnp.stack([ordered[:, 5], ordered[:, 2]], axis=1),
        pool_grad,
        natural_exit[:, 0],
        jnp.transpose(cls_rows, (0, 2, 1)),
        cls_sums,
    )


def solution(mesh):
    in_specs = (
        P("dp", None),
        P("dp", None),
        P(),
        P("dp", None),
        P("dp"),
        P(None, None, "dp", "tensor"),
        P(None, None, "tensor"),
        P(None, "tensor", "dp"),
        P(),
        P(None, "dp", "tensor"),
        P(None, "tensor"),
        P(None, "tensor", "dp"),
        P(),
        P(),
        P(),
        P(None, "dp", None),
        P(),
        P(),
        P(),
    )
    out_specs = (
        P("dp", None),
        P(None, "dp", None),
        P("dp", None),
        P(None, None, "dp", "tensor"),
        P(None, None, "tensor"),
        P(None, "tensor", "dp"),
        P(),
        P(None, "dp", "tensor"),
        P(None, "tensor"),
        P(None, "tensor", "dp"),
        P(),
        P(),
        P(),
        P(None, "dp", None),
        P(),
        P(),
        P(),
    )
    return jax.shard_map(body, mesh=mesh, in_specs=in_specs, out_specs=out_specs, check_vma=False)
```

```python
import functools
import math

import jax
import jax.numpy as jnp
from jax import lax
from jax.experimental import pallas as pl
from jax.experimental.pallas import tpu as pltpu
from jax.sharding import PartitionSpec as P

HEAD = 64
PAIR = 2 * HEAD
STEP = 16

epsilon = 1e-12
highest = lax.Precision.HIGHEST
root_half = 1.0 / math.sqrt(2.0)
inv_root_tau = 1.0 / math.sqrt(2.0 * math.pi)
f32 = jnp.float32
bf16 = jnp.bfloat16

TREE = (2, 6, 3, 7, 0, 4, 1, 5, 9, 13, 11, 15, 8, 12, 10, 14)


def dot(left, right):
    return lax.dot_general(left, right, (((1,), (0,)), ((), ())), preferred_element_type=f32)


def dot_cols(left, right):
    return lax.dot_general(left, right, (((1,), (1,)), ((), ())), preferred_element_type=f32)


def dot_rows(left, right):
    return lax.dot_general(left, right, (((0,), (0,)), ((), ())), preferred_element_type=f32)


def over_rows(count, fn, step=STEP):
    def one(index, carry):
        fn(pl.ds(pl.multiple_of(index * step, step), step))
        return carry

    lax.fori_loop(0, count // step, one, 0)


def norm_rows(values):
    centered = values - jnp.mean(values, axis=1, keepdims=True)
    scaling = lax.rsqrt(jnp.mean(centered * centered, axis=1, keepdims=True) + epsilon)
    return centered * scaling, scaling


def norm_grad(grad, gain, normed, scaling):
    scaled = grad * gain
    mean_grad = jnp.mean(scaled, axis=1, keepdims=True)
    mean_dot = jnp.mean(scaled * normed, axis=1, keepdims=True)
    return scaling * (scaled - mean_grad - normed * mean_dot)


def fetch(pieces, column, held, sems):
    copies = []
    start = 0
    for index, piece in enumerate(pieces):
        rows = piece.shape[0]
        copies.append(
            pltpu.make_async_copy(
                piece.at[:, pl.ds(column, held.shape[1])],
                held.at[pl.ds(start, rows), :],
                sems.at[index],
            )
        )
        start += rows
    for copy in copies:
        copy.start()
    return copies


def finish(copies):
    for copy in copies:
        copy.wait()


def same_segment(ends, batch, rows):
    at_row = lax.broadcasted_iota(jnp.int32, (rows, rows), 0)
    at_col = lax.broadcasted_iota(jnp.int32, (rows, rows), 1)
    seg_row = jnp.zeros((rows, rows), jnp.int32)
    seg_col = jnp.zeros((rows, rows), jnp.int32)
    for slot in range(ends.shape[1] - 1):
        seg_row = seg_row + (at_row >= ends[batch, slot]).astype(jnp.int32)
        seg_col = seg_col + (at_col >= ends[batch, slot]).astype(jnp.int32)
    return seg_row == seg_col


def attention_kernel(*refs, first, count):
    refs = list(refs)
    if first:
        x_in = refs.pop(0)
    else:
        own, other, hidden, vec = refs[:4]
        refs = refs[4:]
    pieces, refs = refs[:count], refs[count:]
    bias, ends = refs[:2]
    refs = refs[2:]
    if first:
        x_low = x_in
    else:
        x_low, x_res = refs[:2]
        refs = refs[2:]
    qkv, probs, mixed, part, held, sems = refs
    copies = fetch(pieces, 0, held, sems)
    total, width = part.shape
    group = mixed.shape[1]
    if not first:

        def norm(rows):
            values = (
                own[rows, :].astype(f32) + other[rows, :].astype(f32) + vec[0:1, :] + hidden[rows, :]
            )
            result = norm_rows(values)[0] * vec[1:2, :] + vec[2:3, :]
            x_res[rows, :] = result
            x_low[rows, :] = result.astype(bf16)

        over_rows(total, norm)
    finish(copies)
    for index in range(3):
        cols = slice(index * group, (index + 1) * group)
        values = dot(x_low[...], held[:, cols])
        if index != 1:
            values = values + bias[index // 2 : index // 2 + 1, :]
        qkv[:, cols] = values.astype(bf16)
    batches = ends.shape[0]
    rows = total // batches
    low_half = lax.broadcasted_iota(jnp.int32, (rows, PAIR), 1) < HEAD
    zero = jnp.zeros((rows, PAIR), bf16)
    for batch in range(batches):
        keep = same_segment(ends, batch, rows)
        span = slice(batch * rows, (batch + 1) * rows)
        for pair in range(group // PAIR):
            query = qkv[span, pair * PAIR : (pair + 1) * PAIR]
            key = qkv[span, group + pair * PAIR : group + (pair + 1) * PAIR]
            value = qkv[span, 2 * group + pair * PAIR : 2 * group + (pair + 1) * PAIR]
            halves = []
            for side in range(2):
                masked = jnp.where(low_half if side == 0 else ~low_half, query, zero)
                scores = dot_cols(masked, key) * HEAD ** (-0.5)
                scores = jnp.where(keep, scores, -1e30)
                weights = jnp.exp(scores - jnp.max(scores, axis=1, keepdims=True))
                prob = weights / jnp.sum(weights, axis=1, keepdims=True)
                head = (batch * (group // PAIR) + pair) * 2 + side
                probs[head * rows : (head + 1) * rows, :] = prob
                halves.append(dot(prob.astype(bf16), value))
            mixed[span, pair * PAIR : (pair + 1) * PAIR] = jnp.where(
                low_half, halves[0], halves[1]
            ).astype(bf16)
    part[...] = dot_cols(mixed[...], held[:, 3 * group : 4 * group]).astype(bf16)


def ffn_kernel(*refs, count):
    refs = list(refs)
    own, other, x_res, vec = refs[:4]
    refs = refs[4:]
    pieces, refs = refs[:count], refs[count:]
    bias, hidden, normed, scale, hidden_low, pre_act, act_low, part = refs[:8]
    held_in, held_down, in_sems, down_sems = refs[8:]
    in_copies = fetch(pieces, 0, held_in, in_sems)
    down_copies = fetch(pieces, held_in.shape[1], held_down, down_sems)
    total = part.shape[0]

    def norm(rows):
        values = (
            own[rows, :].astype(f32)
            + other[rows, :].astype(f32)
            + vec[0:1, :]
            + x_res[rows, :].astype(f32)
        )
        unit, scaling = norm_rows(values)
        result = unit * vec[1:2, :] + vec[2:3, :]
        normed[rows, :] = unit
        scale[rows, :] = scaling
        hidden[rows, :] = result
        hidden_low[rows, :] = result.astype(bf16)

    over_rows(total, norm)
    finish(in_copies)
    pre_act[...] = dot(hidden_low[...], held_in[...]) + bias[...]

    def act(rows):
        values = pre_act[rows, :]
        act_low[rows, :] = (values * (0.5 * (1.0 + lax.erf(values * root_half)))).astype(bf16)

    over_rows(total, act)
    finish(down_copies)
    part[...] = dot_cols(act_low[...], held_down[...]).astype(bf16)


def grads_of(left, right, outs, column=0):
    start = 0
    for out in outs:
        rows = out.shape[0]
        out[:, column : column + right.shape[1]] = dot_rows(
            left[:, start : start + rows], right
        ).astype(bf16)
        start += rows


def exit_kernel(*refs, layer, last, classes):
    refs = list(refs)
    own, other, hidden, vec = refs[:4]
    refs = refs[4:]
    if last:
        cot = refs.pop(0)
    else:
        x_own, x_other, x_direct = refs[:3]
        refs = refs[3:]
    pool_near, pool_far, pool_b, cls_t, cls_b, aux = refs[:6]
    refs = refs[6:]
    if last:
        act_low = refs.pop(0)
    exits, g_c, g_ffn, sums, plain = refs[:5]
    refs = refs[5:]
    if last:
        outs, out_low = refs[:4], refs[4]
        refs = refs[5:]
    else:
        twice_out, both_out = refs[:2]
        refs = refs[2:]
    held, far, near_sems, far_sems, normed, scale = refs[:6]
    if not last:
        out_low = refs[6]
    grad_out = refs[-1]
    total, width = g_c.shape
    half = held.shape[1]
    near_copies = fetch([pool_near], layer * half, held, near_sems)
    far_copies = fetch([pool_far], layer * half, far, far_sems)

    def norm(rows):
        values = (
            own[rows, :].astype(f32) + other[rows, :].astype(f32) + vec[0:1, :] + hidden[rows, :]
        )
        unit, scaling = norm_rows(values)
        normed[rows, :] = unit
        scale[rows, :] = scaling
        out_low[rows, :] = (unit * vec[1:2, :] + vec[2:3, :]).astype(bf16)

    over_rows(total, norm)
    slots = aux.shape[0]
    picks = aux[:, 0:1].astype(jnp.int32)
    valid = aux[:, 1:2]
    chosen = (lax.broadcasted_iota(jnp.int32, (slots, total), 1) == picks).astype(bf16)
    taken = dot(chosen, out_low[...]).astype(bf16)
    finish(near_copies)
    finish(far_copies)
    pooled = jnp.tanh(
        jnp.concatenate([dot(taken, held[...]), dot(taken, far[...])], axis=1) + pool_b[...]
    )
    logits = [
        (jnp.sum(pooled * cls_t[index : index + 1, :], axis=1, keepdims=True)
         + cls_b[0:1, index : index + 1]) * valid
        for index in range(classes)
    ]
    top = functools.reduce(jnp.maximum, logits)
    powers = [jnp.exp(item - top) for item in logits]
    norm_sum = sum(powers[1:], powers[0])
    lane = lax.broadcasted_iota(jnp.int32, exits.shape, 1)
    shown = jnp.zeros(exits.shape, f32)
    grads = []
    for index in range(classes):
        shown = jnp.where(lane == index, logits[index], shown)
        grads.append((powers[index] / norm_sum - aux[:, 2 + index : 3 + index]) * valid)
    exits[...] = shown
    back = grads[0] * cls_t[0:1, :]
    for index in range(1, classes):
        back = back + grads[index] * cls_t[index : index + 1, :]
    grad_z = back * (1.0 - pooled * pooled)
    high = grad_z.astype(bf16)
    rest = (grad_z - high.astype(f32)).astype(bf16)
    both = jnp.concatenate([high, rest], axis=0)
    twice = jnp.concatenate([taken, taken], axis=0)
    if last:
        grads_of(twice, both[:, :half], outs, act_low.shape[1])
    else:
        twice_out[...] = twice
        both_out[...] = both[:, :half]
    pick = dot_cols(both[:, :half], held[...]) + dot_cols(both[:, half:], far[...])
    pick = pick[:slots, :] + pick[slots:, :]
    pick_high = pick.astype(bf16)
    pick_rest = (pick - pick_high.astype(f32)).astype(bf16)
    twice_chosen = jnp.concatenate([chosen, chosen], axis=0)
    grad_out[...] = dot_rows(twice_chosen, jnp.concatenate([pick_high, pick_rest], axis=0))
    sums[...] = jnp.zeros(sums.shape, f32)

    def back_norm(rows):
        if last:
            grad = cot[rows, :].astype(f32)
        else:
            grad = x_own[rows, :].astype(f32) + x_other[rows, :].astype(f32) + x_direct[rows, :]
        grad = grad + grad_out[rows, :]
        unit = normed[rows, :]
        result = norm_grad(grad, vec[1:2, :], unit, scale[rows, :])
        g_c[rows, :] = result
        g_ffn[rows, :] = result.astype(bf16)
        sums[0:1, :] += jnp.sum(result, axis=0, keepdims=True)
        sums[1:2, :] += jnp.sum(grad * unit, axis=0, keepdims=True)
        sums[2:3, :] += jnp.sum(grad, axis=0, keepdims=True)

    over_rows(total, back_norm)
    plain[...] = jnp.zeros(plain.shape, f32)
    plain[0:1, :] = jnp.sum(grad_z, axis=0, keepdims=True)
    spot = lax.broadcasted_iota(jnp.int32, (1, width), 1)
    tail = jnp.zeros((1, width), f32)
    for index in range(classes):
        plain[2 + index : 3 + index, :] = jnp.sum(grads[index] * pooled, axis=0, keepdims=True)
        tail = jnp.where(spot == index, jnp.sum(grads[index], axis=0, keepdims=True), tail)
    plain[1:2, :] = tail
    if last:
        grads_of(g_ffn, act_low[...], outs)


def ffn_back_kernel(*refs, last, count):
    refs = list(refs)
    g_ffn, pre_act = refs[:2]
    refs = refs[2:]
    if not last:
        hidden_low, act_low, twice, both = refs[:4]
        refs = refs[4:]
    pieces, refs = refs[:count], refs[count:]
    sums, part = refs[:2]
    refs = refs[2:]
    if last:
        g_pre = refs.pop(0)
    else:
        outs, refs = refs[:4], refs[4:]
    held_in, held_down, in_sems, down_sems, g_act = refs[:5]
    if not last:
        g_pre = refs[5]
    ff = held_in.shape[1]
    down_copies = fetch(pieces, ff, held_down, down_sems)
    in_copies = fetch(pieces, 0, held_in, in_sems)
    total = part.shape[0]
    finish(down_copies)
    g_act[...] = dot(g_ffn[...], held_down[...])
    sums[...] = jnp.zeros(sums.shape, f32)

    def slope(rows):
        values = pre_act[rows, :]
        cdf = 0.5 * (1.0 + lax.erf(values * root_half))
        pdf = jnp.exp(-0.5 * values * values) * inv_root_tau
        result = (g_act[rows, :] * (cdf + values * pdf)).astype(bf16)
        g_pre[rows, :] = result
        sums[0:1, :] += jnp.sum(result.astype(f32), axis=0, keepdims=True)

    over_rows(total, slope)
    if not last:
        grads_of(g_ffn, act_low[...], outs)
        grads_of(twice, both[...], outs, ff)
        grads_of(hidden_low, g_pre[...], outs, ff + both.shape[1])
    finish(in_copies)
    part[...] = dot_cols(g_pre[...], held_in[...]).astype(bf16)


def attention_back_kernel(*refs, last, count):
    refs = list(refs)
    g_c, own, other, normed, scale, vec = refs[:6]
    refs = refs[6:]
    pieces, refs = refs[:count], refs[count:]
    qkv, probs, mixed, x_low = refs[:4]
    refs = refs[4:]
    if last:
        hidden_low, g_pre = refs[:2]
        refs = refs[2:]
    g_a, part, sums, bias_sums = refs[:4]
    outs, refs = refs[4:8], refs[8:]
    held, sems, g_attn, g_mixed, g_qkv = refs
    copies = fetch(pieces, 0, held, sems)
    total, width = g_c.shape
    group = mixed.shape[1]
    sums[...] = jnp.zeros(sums.shape, f32)

    def back_norm(rows):
        grad = g_c[rows, :] + (own[rows, :].astype(f32) + other[rows, :].astype(f32))
        unit = normed[rows, :]
        result = norm_grad(grad, vec[1:2, :], unit, scale[rows, :])
        g_a[rows, :] = result
        g_attn[rows, :] = result.astype(bf16)
        sums[0:1, :] += jnp.sum(result, axis=0, keepdims=True)
        sums[1:2, :] += jnp.sum(grad * unit, axis=0, keepdims=True)
        sums[2:3, :] += jnp.sum(grad, axis=0, keepdims=True)

    over_rows(total, back_norm)
    finish(copies)
    g_mixed[...] = dot(g_attn[...], held[:, 3 * group : 4 * group]).astype(bf16)
    rows = probs.shape[1]
    batches = total // rows
    low_half = lax.broadcasted_iota(jnp.int32, (rows, PAIR), 1) < HEAD
    zero = jnp.zeros((rows, PAIR), bf16)
    factor = HEAD ** (-0.5)
    for batch in range(batches):
        span = slice(batch * rows, (batch + 1) * rows)
        for pair in range(group // PAIR):
            cols = slice(pair * PAIR, (pair + 1) * PAIR)
            key_cols = slice(group + pair * PAIR, group + (pair + 1) * PAIR)
            value_cols = slice(2 * group + pair * PAIR, 2 * group + (pair + 1) * PAIR)
            query, key, value = qkv[span, cols], qkv[span, key_cols], qkv[span, value_cols]
            grad = g_mixed[span, cols]
            sides = []
            for side in range(2):
                head = (batch * (group // PAIR) + pair) * 2 + side
                prob = probs[head * rows : (head + 1) * rows, :]
                masked = jnp.where(low_half if side == 0 else ~low_half, grad, zero)
                grad_prob = dot_cols(masked, value)
                row_dot = jnp.sum(prob * grad_prob, axis=1, keepdims=True)
                grad_score = (prob * (grad_prob - row_dot)).astype(bf16)
                sides.append(
                    (
                        dot(grad_score, key) * factor,
                        dot_rows(grad_score, query) * factor,
                        dot_rows(prob.astype(bf16), grad),
                    )
                )
            for where_to, near, far in zip((cols, key_cols, value_cols), sides[0], sides[1]):
                g_qkv[span, where_to] = jnp.where(low_half, near, far).astype(bf16)
    part[...] = dot_cols(g_qkv[...], held[:, : 3 * group]).astype(bf16)
    bias_sums[:, :group] = jnp.sum(g_qkv[:, :group].astype(f32), axis=0, keepdims=True)
    bias_sums[:, group:] = jnp.sum(g_qkv[:, 2 * group :].astype(f32), axis=0, keepdims=True)
    column = 0
    if last:
        grads_of(hidden_low, g_pre[...], outs)
        column = g_pre.shape[1]
    grads_of(x_low, g_qkv[...], outs, column)
    grads_of(g_attn, mixed[...], outs, column + 3 * group)


VM = pltpu.VMEM
SM = pltpu.SMEM
ANY = pl.ANY


def launch(kernel, name, ins, outs, scratch):
    specs = [pl.BlockSpec(memory_space=space) for _, space in ins]
    return pl.pallas_call(
        kernel,
        name=name,
        in_specs=specs,
        out_shape=[jax.ShapeDtypeStruct(shape, kind) for shape, kind in outs],
        out_specs=[pl.BlockSpec(memory_space=VM) for _ in outs],
        scratch_shapes=scratch,
    )(*[item for item, _ in ins])


def vm(*items):
    return [(item, VM) for item in items]


def anywhere(items):
    return [(item, ANY) for item in items]


def hop(value, flip, size):
    return lax.ppermute(value, "dp", [(index, index ^ flip) for index in range(size)])


def across(value):
    return lax.ppermute(value, "tensor", [(0, 1), (1, 0)])


def gather_tree(shard, size):
    near = [hop(shard, 4 * step, size) for step in (1, 2, 3)]
    half_a = jnp.concatenate([shard, near[0]], axis=0)
    half_b = jnp.concatenate([near[1], near[2]], axis=0)
    a_x = hop(half_a, 1, size)
    b_y = hop(half_b, 2, size)
    a_y = hop(half_a, 2, size)
    b_x = hop(half_b, 1, size)
    a_xy = hop(a_x, 2, size)
    b_xy = hop(b_y, 1, size)
    return [a_y, a_xy, half_a, a_x, b_x, b_xy, half_b, b_y]


def reduce_tree(parts, size):
    send_a, keep_a, send_b, keep_b = parts
    rows = keep_a.shape[0] // 2
    unit = rows // 2
    got_a = hop(send_a, 2, size)
    got_b = hop(send_b, 1, size)
    next_a = (keep_a[rows:].astype(f32) + got_a[rows:].astype(f32)).astype(bf16)
    next_b = (keep_b[rows:].astype(f32) + got_b[rows:].astype(f32)).astype(bf16)
    far_a = hop(next_a, 1, size)
    far_b = hop(next_b, 2, size)
    sum_a = keep_a[:rows].astype(f32) + got_a[:rows].astype(f32) + far_a.astype(f32)
    sum_b = keep_b[:rows].astype(f32) + got_b[:rows].astype(f32) + far_b.astype(f32)
    z_one = hop(sum_a[unit:].astype(bf16), 4, size)
    z_two = hop(sum_b[:unit].astype(bf16), 8, size)
    z_three = hop(sum_b[unit:].astype(bf16), 12, size)
    return sum_a[:unit] + z_one.astype(f32) + z_two.astype(f32) + z_three.astype(f32)


def onehot(values, count):
    return (jnp.arange(count, dtype=jnp.int32)[:, None] == values[None, :]).astype(bf16)


def move(left, right, rows=False):
    return (dot_rows if rows else dot)(left, right).astype(bf16)


def exact(left, right):
    return jnp.dot(left, right, precision=highest, preferred_element_type=f32)


def body(
    tokens,
    cotangent,
    packing,
    lengths,
    labels,
    w_qkv,
    b_qv,
    w_out,
    b_out,
    w_in,
    b_in,
    w_down,
    b_down,
    norm_gains,
    norm_shifts,
    pool_w,
    pool_b,
    cls_w,
    cls_b,
):
    total, width = tokens.shape
    micro, slots = lengths.shape
    row_count = total // micro
    layers = w_qkv.shape[0]
    classes = cls_w.shape[2]
    group = b_qv.shape[2]
    ff = b_in.shape[1]
    size = lax.axis_size("dp")
    data_index = lax.axis_index("dp")
    tensor_index = lax.axis_index("tensor")
    share = total // size
    half = width // 2
    tree = size == 16 and width % 256 == 0

    def gather(shard):
        if tree:
            return gather_tree(shard, size)
        return [lax.all_gather(shard, "dp", axis=0, tiled=True)]

    def halves(value):
        return lax.dynamic_slice_in_dim(value, tensor_index * half, half, axis=value.ndim - 1)

    attn_w, ffn_w = [], []
    for layer in range(layers):
        shard = [w_qkv[layer, 0], w_qkv[layer, 1], w_qkv[layer, 2], w_out[layer].T]
        if layer == layers - 1:
            shard += [halves(pool_w[item]) for item in range(layers)]
        attn_w.append(gather(jnp.concatenate(shard, axis=1)))
        ffn_w.append(gather(jnp.concatenate([w_in[layer], w_down[layer].T], axis=1)))
    pool_near = jnp.concatenate([piece[:, 4 * group :] for piece in attn_w[-1]], axis=0)
    pool_far = across(pool_near)
    count = len(attn_w[0])

    column = jnp.arange(width, dtype=jnp.int32)
    if tree:
        unit = width // size
        order = jnp.asarray(TREE, jnp.int32) ^ data_index
        natural = jnp.repeat(order, unit) * unit + column % unit
    else:
        natural = column
    shuffle = onehot(natural, width)
    shuffle_half = halves(shuffle.T)

    own_places = lax.dynamic_slice_in_dim(packing, data_index * total, total)
    own_targets = own_places // total
    index = jnp.arange(total, dtype=jnp.int32)
    earlier = (own_targets[:, None] == own_targets[None, :]) & (index[None, :] < index[:, None])
    slot = own_targets * share + jnp.sum(earlier.astype(jnp.int32), axis=1)
    send = onehot(slot, total)
    table = packing.reshape(size, total)
    mine = table // total == data_index
    before = (index[:, None] < index[None, :]).astype(bf16)
    rank = dot(mine.astype(bf16), before).astype(jnp.int32)
    hit = mine[:, None, :] & (rank[:, None, :] == jnp.arange(share, dtype=jnp.int32)[None, :, None])
    places = jnp.sum(jnp.where(hit, (table - data_index * total)[:, None, :], 0), axis=2)
    place = onehot(places.reshape(total), total)

    def swap(value):
        return lax.all_to_all(value, "dp", split_axis=0, concat_axis=0, tiled=True)

    def joined(value):
        far = across(value)
        return jnp.where(
            tensor_index == 0,
            jnp.concatenate([value, far], axis=1),
            jnp.concatenate([far, value], axis=1),
        )

    loaded = jnp.concatenate([halves(tokens), halves(cotangent)], axis=1)
    arrived = move(place, swap(move(send, loaded)))
    far = across(arrived)
    first = jnp.where(tensor_index == 0, arrived, far)
    second = jnp.where(tensor_index == 0, far, arrived)
    packed_tokens = move(jnp.concatenate([first[:, :half], second[:, :half]], axis=1), shuffle)
    packed_cot = move(jnp.concatenate([first[:, half:], second[:, half:]], axis=1), shuffle)

    def unpack(value):
        back = swap(move(place, move(value, shuffle_half), rows=True))
        return joined(move(send, back, rows=True))

    vectors = exact(
        jnp.concatenate(
            [b_out, b_down, norm_gains.reshape(2 * layers, width), norm_shifts.reshape(2 * layers, width)]
        ),
        shuffle.astype(f32),
    )

    def vector_rows(layer, which):
        base = [layer + (0 if which == 0 else layers), 2 * layers + 2 * layer + which, 4 * layers + 2 * layer + which]
        return jnp.concatenate([vectors[item : item + 1] for item in base])

    def own_first(value):
        return jnp.where(tensor_index == 0, value, jnp.roll(value, half, axis=-1))

    ends = jnp.cumsum(lengths, axis=1, dtype=jnp.int32)
    starts = ends - lengths
    picks = jnp.minimum(starts, row_count - 1) + row_count * jnp.arange(micro, dtype=jnp.int32)[:, None]
    label_hot = (labels[:, None] == jnp.arange(classes, dtype=jnp.int32)[None, :]).astype(f32)
    aux = jnp.concatenate(
        [
            picks.reshape(micro * slots, 1).astype(f32),
            (lengths > 0).astype(f32).reshape(micro * slots, 1),
            label_hot,
            jnp.zeros((micro * slots, 126 - classes), f32),
        ],
        axis=1,
    )

    sem = pltpu.SemaphoreType.DMA((count,))
    heads = group // HEAD
    saved = []
    x_res = packed_tokens
    x_low = packed_tokens
    incoming = None
    for layer in range(layers):
        is_first = layer == 0
        outs = [
            ((total, 3 * group), bf16),
            ((micro * heads * row_count, row_count), f32),
            ((total, group), bf16),
            ((total, width), bf16),
        ]
        if is_first:
            ins = vm(packed_tokens)
        else:
            outs = [((total, width), bf16), ((total, width), f32)] + outs
            ins = vm(*incoming)
        result = launch(
            functools.partial(attention_kernel, first=is_first, count=count),
            "attention",
            ins + anywhere(attn_w[layer]) + vm(b_qv[layer]) + [(ends, SM)],
            outs,
            [VM((width, 4 * group), bf16), sem],
        )
        if not is_first:
            x_low, x_res = result[:2]
            result = result[2:]
        qkv, probs, mixed, attn_part = result
        hidden, normed, scale, hidden_low, pre_act, act_low, ffn_part = launch(
            functools.partial(ffn_kernel, count=count),
            "ffn",
            vm(attn_part, across(attn_part), x_res, vector_rows(layer, 0))
            + anywhere(ffn_w[layer])
            + vm(b_in[layer][None]),
            [
                ((total, width), f32),
                ((total, width), f32),
                ((total, 1), f32),
                ((total, width), bf16),
                ((total, ff), f32),
                ((total, ff), bf16),
                ((total, width), bf16),
            ],
            [VM((width, ff), bf16), VM((width, ff), bf16), sem, sem],
        )
        incoming = (ffn_part, across(ffn_part), hidden, vector_rows(layer, 1))
        saved.append((x_low, qkv, probs, mixed, normed, scale, hidden_low, pre_act, act_low, incoming))

    quarter = width // 4
    exit_list = [None] * layers
    sums_list = [None] * layers
    chunks = [None] * layers
    block_out = None
    passed = None
    for layer in reversed(range(layers)):
        x_low, qkv, probs, mixed, normed, scale, hidden_low, pre_act, act_low, incoming = saved[layer]
        is_last = layer == layers - 1
        outs = [
            ((micro * slots, 128), f32),
            ((total, width), f32),
            ((total, width), bf16),
            ((8, width), f32),
            ((8, width), f32),
        ]
        one = pltpu.SemaphoreType.DMA((1,))
        scratch = [VM((width, half), bf16), VM((width, half), bf16), one, one, VM((total, width), f32), VM((total, 1), f32)]
        if is_last:
            outs += [((quarter, ff + half), bf16)] * 4 + [((total, width), bf16)]
        else:
            outs += [((2 * micro * slots, width), bf16), ((2 * micro * slots, half), bf16)]
            scratch.append(VM((total, width), bf16))
        scratch.append(VM((total, width), f32))
        result = launch(
            functools.partial(exit_kernel, layer=layer, last=is_last, classes=classes),
            "exit",
            vm(*incoming)
            + vm(*((packed_cot,) if is_last else passed))
            + anywhere([pool_near, pool_far])
            + vm(own_first(pool_b[layer])[None], own_first(cls_w[layer].T), cls_b[layer][None], aux)
            + (vm(act_low) if is_last else []),
            outs,
            scratch,
        )
        exits, g_c, g_ffn, exit_sums, exit_plain = result[:5]
        scratch = [VM((width, ff), bf16), VM((width, ff), bf16), sem, sem, VM((total, ff), f32)]
        if is_last:
            chunks[layer] = [result[5:9]]
            block_out = unpack(result[9])
            more = []
            outs = [((total, ff), bf16)]
        else:
            more = vm(hidden_low, act_low, *result[5:7])
            outs = [((quarter, 2 * ff + half), bf16)] * 4
            scratch.append(VM((total, ff), bf16))
        back = launch(
            functools.partial(ffn_back_kernel, last=is_last, count=count),
            "ffn_back",
            vm(g_ffn, pre_act) + more + anywhere(ffn_w[layer]),
            [((1, ff), f32), ((total, width), bf16)] + outs,
            scratch,
        )
        in_sums, hidden_part = back[:2]
        if is_last:
            more = vm(hidden_low, back[2])
            wide = 4 * group + ff
        else:
            chunks[layer] = [back[2:]]
            more = []
            wide = 4 * group
        back = launch(
            functools.partial(attention_back_kernel, last=is_last, count=count),
            "attention_back",
            vm(g_c, hidden_part, across(hidden_part), normed, scale, vector_rows(layer, 0))
            + anywhere(attn_w[layer])
            + vm(qkv, probs, mixed, x_low)
            + more,
            [((total, width), f32), ((total, width), bf16), ((8, width), f32), ((1, 2 * group), f32)]
            + [((quarter, wide), bf16)] * 4,
            [
                VM((width, 4 * group), bf16),
                sem,
                VM((total, width), bf16),
                VM((total, group), bf16),
                VM((total, 3 * group), bf16),
            ],
        )
        g_a, x_part, attn_sums, bias_sums = back[:4]
        chunks[layer].append(back[4:])
        passed = (x_part, across(x_part), g_a)
        exit_list[layer] = exits
        sums_list[layer] = (exit_sums, attn_sums, exit_plain, in_sums, bias_sums)
    final = (passed[0].astype(f32) + passed[1].astype(f32) + passed[2]).astype(bf16)
    tokens_grad = unpack(final)

    def reduce_rows(parts):
        if tree:
            return reduce_tree(parts, size)
        return lax.psum_scatter(
            jnp.concatenate(parts, axis=0), "dp", scatter_dimension=0, tiled=True
        ).astype(f32)

    down_list, in_list, attn_list, pool_list = [], [], [], []
    for layer in range(layers):
        first, second = [reduce_rows(parts) for parts in chunks[layer]]
        down_list.append(first[:, :ff].T)
        pool_list.append(first[:, ff : ff + half])
        if layer == layers - 1:
            in_list.append(second[:, :ff])
            attn_list.append(second[:, ff:])
        else:
            in_list.append(first[:, ff + half :])
            attn_list.append(second)
    qkv_grad = jnp.stack(
        [
            jnp.stack([item[:, which * group : (which + 1) * group] for which in range(3)])
            for item in attn_list
        ]
    )
    out_grad = jnp.stack([item[:, 3 * group :].T for item in attn_list])
    in_grad = jnp.stack(in_list)
    down_grad = jnp.stack(down_list)
    pool_grad = joined(jnp.concatenate(pool_list, axis=0))
    pool_grad = pool_grad.reshape(layers, pool_w.shape[1], width)

    ordered, plain = [], []
    for exit_sums, attn_sums, exit_plain, in_sums, bias_sums in sums_list:
        ordered += [exit_sums, attn_sums]
        plain += [exit_plain, in_sums.reshape(ff // width, width), bias_sums]
    ordered = lax.dot_general(
        jnp.concatenate(ordered),
        shuffle.astype(f32),
        (((1,), (1,)), ((), ())),
        precision=highest,
        preferred_element_type=f32,
    )
    vector_sum = jnp.concatenate([ordered] + plain)
    if tree:
        for flip in (1, 2, 4, 8):
            vector_sum = vector_sum + hop(vector_sum, flip, size)
    else:
        vector_sum = lax.psum(vector_sum, "dp")
    ordered, plain = vector_sum[: 16 * layers], vector_sum[16 * layers :]
    each = plain.shape[0] // layers
    plain = plain.reshape(layers, each, width)
    ordered = ordered.reshape(layers, 16, width)
    natural_exit = own_first(plain[:, :4])
    cls_sums = plain[:, 1, :classes]
    cls_rows = natural_exit[:, 2 : 2 + classes]
    in_rows = plain[:, 8 : 8 + ff // width].reshape(layers, ff)
    bias_rows = plain[:, 8 + ff // width].reshape(layers, 2, group)
    return (
        block_out,
        jnp.stack(exit_list)[:, :, :classes],
        tokens_grad,
        qkv_grad,
        bias_rows,
        out_grad,
        ordered[:, 8],
        in_grad,
        in_rows,
        down_grad,
        ordered[:, 0],
        jnp.stack([ordered[:, 9], ordered[:, 1]], axis=1),
        jnp.stack([ordered[:, 10], ordered[:, 2]], axis=1),
        pool_grad,
        natural_exit[:, 0],
        jnp.transpose(cls_rows, (0, 2, 1)),
        cls_sums,
    )


def solution(mesh):
    in_specs = (
        P("dp", None),
        P("dp", None),
        P(),
        P("dp", None),
        P("dp"),
        P(None, None, "dp", "tensor"),
        P(None, None, "tensor"),
        P(None, "tensor", "dp"),
        P(),
        P(None, "dp", "tensor"),
        P(None, "tensor"),
        P(None, "tensor", "dp"),
        P(),
        P(),
        P(),
        P(None, "dp", None),
        P(),
        P(),
        P(),
    )
    out_specs = (
        P("dp", None),
        P(None, "dp", None),
        P("dp", None),
        P(None, None, "dp", "tensor"),
        P(None, None, "tensor"),
        P(None, "tensor", "dp"),
        P(),
        P(None, "dp", "tensor"),
        P(None, "tensor"),
        P(None, "tensor", "dp"),
        P(),
        P(),
        P(),
        P(None, "dp", None),
        P(),
        P(),
        P(),
    )
    return jax.shard_map(body, mesh=mesh, in_specs=in_specs, out_specs=out_specs, check_vma=False)
```
